32 devices in a mesh: dp: 4 (over x, core), group: 8 (over z, y).
Axes of the slice: x: 2, y: 2, z: 4, core: 2. Of those that a mesh axis runs over, the one named last changes fastest.
Arguments:
- features: bfloat16 [8192, 3072], P(('dp', 'group')), may hold values from -6 to 6
- target_embed: bfloat16 [8192, 256], P(('dp', 'group')), may hold values from -80 to 80
- proj_weight: bfloat16 [3072, 256], replicated, may hold values from -0.109375 to 0.109375
- prototypes: float32 [2048, 256], replicated, may hold values from -20 to 20
Outputs:
- grad_feat: bfloat16 [8192, 3072], P(('dp', 'group'))
- grad_proj: float32 [3072, 256], P('group')
- grad_protos: float32 [2048, 256], replicated
The draws below stay inside these ranges and needn't reach their ends.
All inputs are finite; a program needn't handle non-finite values.
Results may differ from the reference program's by a relative error of at most 0.0067.
Values sent between devices are 32-bit elements; how exact they have to be, the bound alone decides.
A program may use at most 64 MiB of HBM per device.

```python
import math
import jax
import jax.numpy as jnp
from jax import lax

FR_DEV = 256
FEAT = 3072
PW = 256
NP = 2048
SWEEPS = 3
FRAMES = 8192
N_DP = 4
N_GROUP = 8


def common_centers(key):
    centers = jax.random.normal(jax.random.fold_in(key, 7001), (32, PW), jnp.float32)
    return jnp.clip(centers, -4.0, 4.0)


def draw_target_embed(key, part):
    centers = common_centers(key)
    own_key = jax.random.fold_in(key, 101)
    key_one, key_two, key_three, key_jitter, key_scale = jax.random.split(own_key, 5)
    labels = jnp.minimum(jax.random.randint(key_one, (FRAMES,), 0, 32), jax.random.randint(key_two, (FRAMES,), 0, 32))
    labels = jnp.minimum(labels, jax.random.randint(key_three, (FRAMES,), 0, 32))
    jitter = jnp.clip(jax.random.normal(key_jitter, (FRAMES, PW), jnp.float32), -4.0, 4.0)
    row_scale = jnp.exp(jax.random.uniform(key_scale, (FRAMES, 1), jnp.float32, 0.0, math.log(4.0)))
    values = (centers[labels] + jitter) * row_scale
    return values.astype(jnp.bfloat16)


def draw_prototypes(key, part):
    centers = common_centers(key)
    own_key = jax.random.fold_in(key, 202)
    key_pick, key_jitter, key_scale = jax.random.split(own_key, 3)
    picks = jax.random.randint(key_pick, (NP,), 0, 64)
    near = picks < 32
    anchor = centers[jnp.remainder(picks, 32)]
    jitter = jnp.clip(jax.random.normal(key_jitter, (NP, PW), jnp.float32), -4.0, 4.0)
    row_scale = jnp.exp(jax.random.uniform(key_scale, (NP, 1), jnp.float32, math.log(0.5), math.log(2.0)))
    values = jnp.where(near[:, None], anchor + jitter, 1.4 * jitter) * row_scale
    return values.astype(jnp.float32)


def block_levels(rng, shape, cuts, least, high):
    def one(axis_at, shards_of):
        draws = jax.random.uniform(jax.random.fold_in(jax.random.fold_in(rng, 6), axis_at), (shards_of,), jnp.float32, least / len(cuts), high / len(cuts))
        return jnp.repeat(jnp.exp(draws), shape[axis_at] // shards_of).reshape((-1,) + (1,) * (len(shape) - axis_at - 1))

    level = one(*cuts[0])
    for cut in cuts[1:]:
        level = level * one(*cut)
    return level


def bell_draw(key, shape, scale, limit, cuts=(), held_as=jnp.bfloat16):
    gain = block_levels(key, shape, cuts, -0.22, 0.18) if cuts else 1.0
    drawn = jax.random.normal(key, shape, jnp.float32) * scale * gain
    return jnp.minimum(jnp.maximum(drawn, -limit), limit).astype(held_as)


def setup_inputs(seed: int = 0) -> dict:
    keys = jax.random.split(jax.random.key(seed), 5)
    features = bell_draw(keys[0], (FRAMES, FEAT), 1.0, 6.0, ((0, 32),))
    target_embed = draw_target_embed(jax.random.fold_in(keys[4], 71), 0)
    proj_weight = bell_draw(keys[2], (FEAT, PW), FEAT ** -0.5, 0.109375)
    prototypes = draw_prototypes(jax.random.fold_in(keys[4], 71), 0)
    return dict(features=features, target_embed=target_embed, proj_weight=proj_weight, prototypes=prototypes)


def normalize(values):
    return values * lax.rsqrt(lax.optimization_barrier(jnp.sum(values * values, axis=-1, keepdims=True)) + 1e-06)

def rownorm(matrix):
    return matrix / lax.optimization_barrier(jnp.sum(matrix, axis=1, keepdims=True))

def reference(features, target_embed, proj_weight, prototypes):
    unit_protos, proto_back = jax.vjp(normalize, prototypes)
    proto_b = unit_protos.astype(jnp.bfloat16)
    blocks = N_DP * N_GROUP
    feat_blocks = features.reshape(blocks, FR_DEV, FEAT)
    tgt_blocks = target_embed.reshape(blocks, FR_DEV, PW)

    def kernel(target):
        target_b = normalize(target.astype(jnp.float32)).astype(jnp.bfloat16)
        scores = jnp.dot(target_b, proto_b.T, preferred_element_type=jnp.float32)
        return jnp.exp(scores * (1.0 / 0.05))
    weights = jnp.ones((NP,), jnp.float32)
    for sweep in range(SWEEPS):

        def column(carry, target, scale=weights):
            return (carry + lax.optimization_barrier(jnp.sum(rownorm(kernel(target) * scale), axis=0)), None)
        colsum, unused = lax.scan(column, jnp.zeros((NP,), jnp.float32), tgt_blocks)
        weights = weights / colsum

    def final(carry, pieces):
        unit_sum, proj_sum = carry
        feat, target = pieces
        plan = rownorm(kernel(target) * weights)
        hidden = jnp.dot(feat, proj_weight, preferred_element_type=jnp.float32)
        embed, embed_back = jax.vjp(normalize, hidden)
        embed_b = embed.astype(jnp.bfloat16)
        online = jnp.dot(embed_b, proto_b.T, preferred_element_type=jnp.float32)
        prob = jax.nn.softmax(online * (1.0 / 0.1), axis=1)
        grad_scores = ((prob - plan) * (1.0 / 0.1)).astype(jnp.bfloat16)
        unit_sum = unit_sum + lax.dot_general(grad_scores, embed_b, (((0,), (0,)), ((), ())), preferred_element_type=jnp.float32)
        grad_embed = jnp.dot(grad_scores, proto_b, preferred_element_type=jnp.float32)
        grad_hidden = embed_back(grad_embed)[0].astype(jnp.bfloat16)
        grad_feat = lax.dot_general(grad_hidden, proj_weight, (((1,), (1,)), ((), ())), preferred_element_type=jnp.float32).astype(jnp.bfloat16)
        proj_sum = proj_sum + lax.dot_general(feat, grad_hidden, (((0,), (0,)), ((), ())), preferred_element_type=jnp.float32)
        return ((unit_sum, proj_sum), grad_feat)
    start = (jnp.zeros((NP, PW), jnp.float32), jnp.zeros((FEAT, PW), jnp.float32))
    (grad_unit, grad_proj), feat_grads = lax.scan(final, start, (feat_blocks, tgt_blocks))
    grad_protos = proto_back(grad_unit)[0]
    return (feat_grads.reshape(FRAMES, FEAT), grad_proj, grad_protos)
```

```python
import functools

import jax
import jax.numpy as jnp
from jax import lax
from jax.experimental import pallas as pl
from jax.experimental.pallas import tpu as pltpu
from jax.sharding import PartitionSpec as P

SWEEPS = 3
MESH = pl.DeviceIdType.MESH
F32 = jnp.float32
BF16 = jnp.bfloat16


def normalize(values):
    return values * lax.rsqrt(jnp.sum(values * values, axis=-1, keepdims=True) + 1e-06)


def inv_norm(values):
    return lax.rsqrt(jnp.sum(values * values, axis=-1, keepdims=True) + 1e-06)


def dot(a, b, ca, cb):
    return lax.dot_general(a, b, (((ca,), (cb,)), ((), ())), preferred_element_type=F32)


def others(n, body):
    if n <= 8:
        for k in range(1, n):
            body(k)
    else:
        lax.fori_loop(1, n, lambda k, c: (body(k), c)[1], 0)


def peer_of(me, k, n):
    return lax.rem(me + k, n)


def scores_kernel(
    n_dp, n_group, feat, target, proj, protos, gs_out, embed_out, gh_out,
    kern, proto_b, slots_d, slots_g, w, hid, send_d, recv_d, send_g, recv_g,
):
    d = lax.axis_index("dp")
    g = lax.axis_index("group")
    barrier = pltpu.get_barrier_semaphore()
    others(n_dp, lambda k: pl.semaphore_signal(
        barrier, inc=1, device_id=(peer_of(d, k, n_dp), g), device_id_type=MESH))
    others(n_group, lambda k: pl.semaphore_signal(
        barrier, inc=1, device_id=(d, peer_of(g, k, n_group)), device_id_type=MESH))

    def copy_d(s, k, owner, peer):
        return pltpu.make_async_remote_copy(
            src_ref=slots_d.at[s, owner], dst_ref=slots_d.at[s, owner],
            send_sem=send_d.at[s, k], recv_sem=recv_d.at[s, owner],
            device_id=(peer, g), device_id_type=MESH)

    def copy_g(s, k, owner, peer):
        return pltpu.make_async_remote_copy(
            src_ref=slots_g.at[s, owner], dst_ref=slots_g.at[s, owner],
            send_sem=send_g.at[s, k], recv_sem=recv_g.at[s, owner],
            device_id=(d, peer), device_id_type=MESH)

    proto_b[...] = normalize(protos[...]).astype(BF16)
    target_b = normalize(target[...].astype(F32)).astype(BF16)
    kern[...] = jnp.exp(dot(target_b, proto_b[...], 1, 1) * (1.0 / 0.05))
    w[...] = jnp.ones_like(w)
    for s in range(SWEEPS):
        row = jnp.sum(kern[...] * w[...], axis=1, keepdims=True)
        slots_d[s, d] = jnp.sum(kern[...] * (1.0 / row), axis=0, keepdims=True)
        if s == 0:
            pl.semaphore_wait(barrier, n_dp - 1 + n_group - 1)
        others(n_dp, lambda k: copy_d(s, k, d, peer_of(d, k, n_dp)).start())
        if s == 0:
            hid[...] = dot(feat[...], proj[...], 1, 0)
        others(n_dp, lambda k: copy_d(s, k, peer_of(d, k, n_dp), d).wait_recv())
        slots_g[s, g] = jnp.sum(slots_d[s], axis=0)
        others(n_group, lambda k: copy_g(s, k, g, peer_of(g, k, n_group)).start())
        if s == 0:
            embed_out[...] = (hid[...] * inv_norm(hid[...])).astype(BF16)
        others(n_group, lambda k: copy_g(s, k, peer_of(g, k, n_group), g).wait_recv())
        w[...] = 1.0 / jnp.sum(slots_g[s], axis=0)
    plan = kern[...] * w[...]
    plan = plan / jnp.sum(plan, axis=1, keepdims=True)
    prob = jnp.exp(dot(embed_out[...], proto_b[...], 1, 1) * (1.0 / 0.1))
    prob = prob / jnp.sum(prob, axis=1, keepdims=True)
    gs_out[...] = ((prob - plan) * (1.0 / 0.1)).astype(BF16)
    ge = dot(gs_out[...], proto_b[...], 1, 0)
    scale = inv_norm(hid[...])
    embed = hid[...] * scale
    gh = scale * (ge - embed * jnp.sum(embed * ge, axis=-1, keepdims=True))
    gh_out[...] = gh.astype(BF16)
    for s in range(SWEEPS):
        others(n_dp, lambda k: copy_d(s, k, d, peer_of(d, k, n_dp)).wait_send())
        others(n_group, lambda k: copy_g(s, k, g, peer_of(g, k, n_group)).wait_send())


def scores(n_dp, n_group, features, target_embed, proj_weight, prototypes):
    rows = features.shape[0]
    count, width = prototypes.shape
    vmem = pl.BlockSpec(memory_space=pltpu.VMEM)
    return pl.pallas_call(
        functools.partial(scores_kernel, n_dp, n_group),
        out_shape=(
            jax.ShapeDtypeStruct((rows, count), BF16),
            jax.ShapeDtypeStruct((rows, width), BF16),
            jax.ShapeDtypeStruct((rows, width), BF16),
        ),
        in_specs=[vmem] * 4,
        out_specs=(vmem,) * 3,
        scratch_shapes=[
            pltpu.VMEM((rows, count), F32),
            pltpu.VMEM((count, width), BF16),
            pltpu.VMEM((SWEEPS, n_dp, 1, count), F32),
            pltpu.VMEM((SWEEPS, n_group, 1, count), F32),
            pltpu.VMEM((1, count), F32),
            pltpu.VMEM((rows, width), F32),
            pltpu.SemaphoreType.DMA((SWEEPS, n_dp)),
            pltpu.SemaphoreType.DMA((SWEEPS, n_dp)),
            pltpu.SemaphoreType.DMA((SWEEPS, n_group)),
            pltpu.SemaphoreType.DMA((SWEEPS, n_group)),
        ],
        compiler_params=pltpu.CompilerParams(
            collective_id=0, has_side_effects=True, vmem_limit_bytes=48 << 20),
        name="scores",
    )(features, target_embed, proj_weight, prototypes)


def sums_kernel(
    n_dp, n_group, gs, embed, feat, gh, proj, unit, pout, gfeat,
    ub, uc, ux, uy, uz, pb, pc, py, pz, px, sem_s, sem_r,
):
    nx, nz = n_dp // 2, n_group // 2
    dp = lax.axis_index("dp")
    grp = lax.axis_index("group")
    x, c = dp // 2, lax.rem(dp, 2)
    z, y = grp // 2, lax.rem(grp, 2)
    count, feats = gs.shape[1], feat.shape[1]

    def at_c(i):
        return (x * 2 + i, grp)

    def at_x(i):
        return (i * 2 + c, grp)

    def at_y(i):
        return (dp, z * 2 + i)

    def at_z(i):
        return (dp, i * 2 + y)

    axes = {"c": (at_c, c, 2), "x": (at_x, x, nx), "y": (at_y, y, 2), "z": (at_z, z, nz)}
    barrier = pltpu.get_barrier_semaphore()
    total = 0
    for at, me, n in axes.values():
        total += n - 1
        for k in range(1, n):
            pl.semaphore_signal(
                barrier, inc=1, device_id=at(peer_of(me, k, n)), device_id_type=MESH)

    base = {}
    sends = []

    def stage(name, axis, src_of, dst_of):
        at, me, n = axes[axis]
        first = base.setdefault(name, sum(v for _, v in used))
        used.append((name, n))

        def make(k, to, sender, peer):
            return pltpu.make_async_remote_copy(
                src_ref=src_of(to), dst_ref=dst_of(sender),
                send_sem=sem_s.at[first + k], recv_sem=sem_r.at[first + sender],
                device_id=at(peer), device_id_type=MESH)

        out = [make(k, peer_of(me, k, n), me, peer_of(me, k, n)) for k in range(1, n)]
        for copy in out:
            copy.start()
        sends.extend(out)

        def wait():
            for k in range(1, n):
                other = peer_of(me, k, n)
                make(k, me, other, other).wait_recv()
        return wait

    used = []

    def land(buf, axis):
        n = axes[axis][2]
        return lambda j: buf.at[j]

    def rows(ref, index, size):
        return ref.at[pl.ds(pl.multiple_of(index * size, size), size)]

    half = count // 2
    r_x, r_y, r_z = half // nx, half // nx // 2, half // nx // 2 // nz

    def unit_half(i):
        cols = pl.ds(pl.multiple_of(i * half, half), half)
        ub[i] = dot(gs[:, cols], embed[...], 0, 0)

    unit_half(1 - c)
    pl.semaphore_wait(barrier, total)
    w_uc = stage("uc", "c", lambda i: ub.at[i], lambda j: uc)
    unit_half(c)

    block = feats // n_group
    hb = block // 2
    hx = hb // nx
    for i in range(n_group):
        part = dot(feat[:, i * block:(i + 1) * block], gh[...], 0, 0)
        for j in range(2):
            pb[j, i % 2, i // 2] = part[j * hb:(j + 1) * hb]
    w_pc = stage("pc", "c", lambda i: pb.at[i], lambda j: pc)

    w_uc()
    ub[c] += uc[...]
    mine = ub.at[c]
    w_ux = stage("ux", "x", lambda i: rows(mine, i, r_x), lambda j: ux.at[j])
    w_pc()
    pb[c] += pc[...]
    w_py = stage("py", "y", lambda i: pb.at[c, i], lambda j: py)
    gfeat[...] = dot(gh[...], proj[...], 1, 1).astype(BF16)

    def add_all(dst, buf, axis):
        _, me, n = axes[axis]
        value = dst[...]
        for k in range(1, n):
            value = value + buf[peer_of(me, k, n)]
        dst[...] = value

    w_ux()
    ux_me = rows(mine, x, r_x)
    add_all(ux_me, ux, "x")
    w_uy = stage("uy", "y", lambda i: rows(ux_me, i, r_y), lambda j: uy)
    w_py()
    pb[c, y] += py[...]
    w_pz = stage("pz", "z", lambda i: pb.at[c, y, i], lambda j: pz.at[j])
    w_uy()
    uy_me = rows(ux_me, y, r_y)
    uy_me[...] += uy[...]
    w_uz = stage("uz", "z", lambda i: rows(uy_me, i, r_z), lambda j: uz.at[j])
    w_uz()
    def out_c(i):
        return rows(unit, i, half)

    def out_x(i):
        return rows(out_c(c), i, r_x)

    def out_y(i):
        return rows(out_x(x), i, r_y)

    def out_z(i):
        return rows(out_y(y), i, r_z)

    value = rows(uy_me, z, r_z)[...]
    for k in range(1, nz):
        value = value + uz[peer_of(z, k, nz)]
    out_z(z)[...] = value
    g_uz = stage("gz", "z", lambda i: out_z(z), lambda j: out_z(j))
    g_uz()
    g_uy = stage("gy", "y", lambda i: out_y(y), lambda j: out_y(j))
    w_pz()
    pz_me = pb.at[c, y, z]
    add_all(pz_me, pz, "z")
    w_px = stage("px", "x", lambda i: rows(pz_me, i, hx), lambda j: px.at[j])
    g_uy()
    g_ux = stage("gx", "x", lambda i: out_x(x), lambda j: out_x(j))
    w_px()

    def pout_c(i):
        return rows(pout, i, hb)

    def pout_x(i):
        return rows(pout_c(c), i, hx)

    value = rows(pz_me, x, hx)[...]
    for k in range(1, nx):
        value = value + px[peer_of(x, k, nx)]
    pout_x(x)[...] = value
    g_px = stage("hx", "x", lambda i: pout_x(x), lambda j: pout_x(j))
    g_ux()
    g_uc = stage("gc", "c", lambda i: out_c(c), lambda j: out_c(j))
    g_px()
    g_pc = stage("hc", "c", lambda i: pout_c(c), lambda j: pout_c(j))
    g_uc()
    g_pc()
    for copy in sends:
        copy.wait_send()


def sums(n_dp, n_group, grad_scores, embed_b, features, grad_hidden, proj_weight):
    nx, nz = n_dp // 2, n_group // 2
    count, feats, width = grad_scores.shape[1], features.shape[1], embed_b.shape[1]
    half = count // 2
    r_x = half // nx
    r_y = r_x // 2
    r_z = r_y // nz
    hb = feats // n_group // 2
    hx = hb // nx
    vmem = pl.BlockSpec(memory_space=pltpu.VMEM)
    n_sem = 16 * max(2, nx, nz)
    return pl.pallas_call(
        functools.partial(sums_kernel, n_dp, n_group),
        out_shape=(
            jax.ShapeDtypeStruct((count, width), F32),
            jax.ShapeDtypeStruct((feats // n_group, width), F32),
            jax.ShapeDtypeStruct(features.shape, BF16),
        ),
        in_specs=[vmem] * 5,
        out_specs=(vmem,) * 3,
        scratch_shapes=[
            pltpu.VMEM((2, half, width), F32),
            pltpu.VMEM((half, width), F32),
            pltpu.VMEM((nx, r_x, width), F32),
            pltpu.VMEM((r_y, width), F32),
            pltpu.VMEM((nz, r_z, width), F32),
            pltpu.VMEM((2, 2, nz, hb, width), F32),
            pltpu.VMEM((2, nz, hb, width), F32),
            pltpu.VMEM((nz, hb, width), F32),
            pltpu.VMEM((nz, hb, width), F32),
            pltpu.VMEM((nx, hx, width), F32),
            pltpu.SemaphoreType.DMA((n_sem,)),
            pltpu.SemaphoreType.DMA((n_sem,)),
        ],
        compiler_params=pltpu.CompilerParams(
            collective_id=1, has_side_effects=True, vmem_limit_bytes=48 << 20),
        name="sums",
    )(grad_scores, embed_b, features, grad_hidden, proj_weight)


def plain_sums(grad_scores, embed_b, features, grad_hidden, proj_weight):
    grad_unit = lax.psum(dot(grad_scores, embed_b, 0, 0), ("dp", "group"))
    grad_feat = dot(grad_hidden, proj_weight, 1, 1).astype(BF16)
    part = lax.psum_scatter(
        dot(features, grad_hidden, 0, 0), "group", scatter_dimension=0, tiled=True)
    return grad_unit, lax.psum(part, "dp"), grad_feat


def solution(mesh):
    n_dp, n_group = mesh.shape["dp"], mesh.shape["group"]

    def local(features, target_embed, proj_weight, prototypes):
        grad_scores, embed_b, grad_hidden = scores(
            n_dp, n_group, features, target_embed, proj_weight, prototypes)
        args = (grad_scores, embed_b, features, grad_hidden, proj_weight)
        unit = 8 * n_dp * n_group
        even = n_dp % 2 == 0 and n_group % 2 == 0
        if even and prototypes.shape[0] % unit == 0 and features.shape[1] % unit == 0:
            grad_unit, grad_proj, grad_feat = sums(n_dp, n_group, *args)
        else:
            grad_unit, grad_proj, grad_feat = plain_sums(*args)
        scale = inv_norm(prototypes)
        unit_protos = prototypes * scale
        along = jnp.sum(unit_protos * grad_unit, axis=-1, keepdims=True)
        grad_protos = (grad_unit - unit_protos * along) * scale
        return (grad_feat, grad_proj, grad_protos)

    return jax.shard_map(
        local,
        mesh=mesh,
        in_specs=(P(("dp", "group"), None), P(("dp", "group"), None), P(), P()),
        out_specs=(P(("dp", "group"), None), P("group", None), P()),
        check_vma=False,
    )
```

```python
import functools

import jax
import jax.numpy as jnp
from jax import lax
from jax.experimental import pallas as pl
from jax.experimental.pallas import tpu as pltpu
from jax.sharding import PartitionSpec as P

SWEEPS = 3
MESH = pl.DeviceIdType.MESH
F32 = jnp.float32
BF16 = jnp.bfloat16


def normalize(values):
    return values * lax.rsqrt(jnp.sum(values * values, axis=-1, keepdims=True) + 1e-06)


def inv_norm(values):
    return lax.rsqrt(jnp.sum(values * values, axis=-1, keepdims=True) + 1e-06)


def dot(a, b, ca, cb):
    return lax.dot_general(a, b, (((ca,), (cb,)), ((), ())), preferred_element_type=F32)


def others(n, body):
    if n <= 8:
        for k in range(1, n):
            body(k)
    else:
        lax.fori_loop(1, n, lambda k, c: (body(k), c)[1], 0)


def peer_of(me, k, n):
    return lax.rem(me + k, n)


def scores_kernel(
    n_dp, n_group, feat, target, proj, protos, gs_out, embed_out, gh_out,
    kern, proto_b, slots_d, slots_g, w, hid, send_d, recv_d, send_g, recv_g,
):
    d = lax.axis_index("dp")
    g = lax.axis_index("group")
    barrier = pltpu.get_barrier_semaphore()
    others(n_dp, lambda k: pl.semaphore_signal(
        barrier, inc=1, device_id=(peer_of(d, k, n_dp), g), device_id_type=MESH))
    others(n_group, lambda k: pl.semaphore_signal(
        barrier, inc=1, device_id=(d, peer_of(g, k, n_group)), device_id_type=MESH))

    def copy_d(s, k, owner, peer):
        return pltpu.make_async_remote_copy(
            src_ref=slots_d.at[s, owner], dst_ref=slots_d.at[s, owner],
            send_sem=send_d.at[s, k], recv_sem=recv_d.at[s, owner],
            device_id=(peer, g), device_id_type=MESH)

    def copy_g(s, k, owner, peer):
        return pltpu.make_async_remote_copy(
            src_ref=slots_g.at[s, owner], dst_ref=slots_g.at[s, owner],
            send_sem=send_g.at[s, k], recv_sem=recv_g.at[s, owner],
            device_id=(d, peer), device_id_type=MESH)

    proto_b[...] = normalize(protos[...]).astype(BF16)
    target_b = normalize(target[...].astype(F32)).astype(BF16)
    kern[...] = jnp.exp(dot(target_b, proto_b[...], 1, 1) * (1.0 / 0.05))
    w[...] = jnp.ones_like(w)
    for s in range(SWEEPS):
        row = jnp.sum(kern[...] * w[...], axis=1, keepdims=True)
        slots_d[s, d] = jnp.sum(kern[...] * (1.0 / row), axis=0, keepdims=True)
        if s == 0:
            pl.semaphore_wait(barrier, n_dp - 1 + n_group - 1)
        others(n_dp, lambda k: copy_d(s, k, d, peer_of(d, k, n_dp)).start())
        if s == 0:
            hid[...] = dot(feat[...], proj[...], 1, 0)
        others(n_dp, lambda k: copy_d(s, k, peer_of(d, k, n_dp), d).wait_recv())
        slots_g[s, g] = jnp.sum(slots_d[s], axis=0)
        others(n_group, lambda k: copy_g(s, k, g, peer_of(g, k, n_group)).start())
        if s == 0:
            embed_out[...] = (hid[...] * inv_norm(hid[...])).astype(BF16)
        others(n_group, lambda k: copy_g(s, k, peer_of(g, k, n_group), g).wait_recv())
        w[...] = 1.0 / jnp.sum(slots_g[s], axis=0)
    plan = kern[...] * w[...]
    plan = plan / jnp.sum(plan, axis=1, keepdims=True)
    prob = jnp.exp(dot(embed_out[...], proto_b[...], 1, 1) * (1.0 / 0.1))
    prob = prob / jnp.sum(prob, axis=1, keepdims=True)
    gs_out[...] = ((prob - plan) * (1.0 / 0.1)).astype(BF16)
    ge = dot(gs_out[...], proto_b[...], 1, 0)
    scale = inv_norm(hid[...])
    embed = hid[...] * scale
    gh = scale * (ge - embed * jnp.sum(embed * ge, axis=-1, keepdims=True))
    gh_out[...] = gh.astype(BF16)
    for s in range(SWEEPS):
        others(n_dp, lambda k: copy_d(s, k, d, peer_of(d, k, n_dp)).wait_send())
        others(n_group, lambda k: copy_g(s, k, g, peer_of(g, k, n_group)).wait_send())


def scores(n_dp, n_group, features, target_embed, proj_weight, prototypes):
    rows = features.shape[0]
    count, width = prototypes.shape
    vmem = pl.BlockSpec(memory_space=pltpu.VMEM)
    return pl.pallas_call(
        functools.partial(scores_kernel, n_dp, n_group),
        out_shape=(
            jax.ShapeDtypeStruct((rows, count), BF16),
            jax.ShapeDtypeStruct((rows, width), BF16),
            jax.ShapeDtypeStruct((rows, width), BF16),
        ),
        in_specs=[vmem] * 4,
        out_specs=(vmem,) * 3,
        scratch_shapes=[
            pltpu.VMEM((rows, count), F32),
            pltpu.VMEM((count, width), BF16),
            pltpu.VMEM((SWEEPS, n_dp, 1, count), F32),
            pltpu.VMEM((SWEEPS, n_group, 1, count), F32),
            pltpu.VMEM((1, count), F32),
            pltpu.VMEM((rows, width), F32),
            pltpu.SemaphoreType.DMA((SWEEPS, n_dp)),
            pltpu.SemaphoreType.DMA((SWEEPS, n_dp)),
            pltpu.SemaphoreType.DMA((SWEEPS, n_group)),
            pltpu.SemaphoreType.DMA((SWEEPS, n_group)),
        ],
        compiler_params=pltpu.CompilerParams(
            collective_id=0, has_side_effects=True, vmem_limit_bytes=48 << 20),
        name="scores",
    )(features, target_embed, proj_weight, prototypes)


UNIT_ORDERS = ("cxyz", "cyxz", "cxyz", "cyxz")
PROJ_ORDERS = ("cyzx", "cxzy", "cyzx", "cxzy")


def sums_kernel(
    n_dp, n_group, gs, embed, feat, gh, proj, unit, pout, gfeat,
    ub, pb, landing, sem_s, sem_r,
):
    nx, nz = n_dp // 2, n_group // 2
    dp = lax.axis_index("dp")
    grp = lax.axis_index("group")
    x, c = dp // 2, lax.rem(dp, 2)
    z, y = grp // 2, lax.rem(grp, 2)
    axes = {
        "c": (lambda i: (x * 2 + i, grp), c, 2),
        "x": (lambda i: (i * 2 + c, grp), x, nx),
        "y": (lambda i: (dp, z * 2 + i), y, 2),
        "z": (lambda i: (dp, i * 2 + y), z, nz),
    }
    barrier = pltpu.get_barrier_semaphore()
    total = 0
    for at, me, n in axes.values():
        total += n - 1
        for k in range(1, n):
            pl.semaphore_signal(
                barrier, inc=1, device_id=at(peer_of(me, k, n)), device_id_type=MESH)

    used = {"sem": 0, "row": 0}
    sends = []

    def take(what, amount):
        first = used[what]
        used[what] += amount
        return first

    def start(axis, src_of, dst_of):
        at, me, n = axes[axis]
        first = take("sem", n)

        def make(k, to, sender, peer):
            return pltpu.make_async_remote_copy(
                src_ref=src_of(to), dst_ref=dst_of(sender),
                send_sem=sem_s.at[first + k], recv_sem=sem_r.at[first + sender],
                device_id=at(peer), device_id_type=MESH)

        for k in range(1, n):
            copy = make(k, peer_of(me, k, n), me, peer_of(me, k, n))
            copy.start()
            sends.append(copy)

        def wait():
            for k in range(1, n):
                other = peer_of(me, k, n)
                make(k, me, other, other).wait_recv()
        return wait

    def piece(ref, base, size):
        return ref.at[pl.ds(pl.multiple_of(base, 8), size)]

    def scatter(order, buf, base, size, out, out_base, gathered):
        for step, axis in enumerate(order):
            _, me, n = axes[axis]
            size //= n
            low, slots = base, take("row", n * size)
            wait = start(
                axis,
                lambda i, low=low, size=size: piece(buf, low + i * size, size),
                lambda j, slots=slots, size=size: piece(landing, slots + j * size, size))
            yield
            wait()
            base = low + me * size
            value = piece(buf, base, size)[...]
            for k in range(1, n):
                value = value + piece(landing, slots + peer_of(me, k, n) * size, size)[...]
            last = step == len(order) - 1
            piece(out if last else buf, out_base if last else base, size)[...] = value
        base = out_base
        for axis in gathered:
            _, me, n = axes[axis]
            low = base - me * size
            wait = start(
                axis,
                lambda i, base=base, size=size: piece(out, base, size),
                lambda j, low=low, size=size: piece(out, low + j * size, size))
            yield
            wait()
            base, size = low, size * n

    where = {"c": c, "x": x, "y": y, "z": z}
    count, feats = gs.shape[1], feat.shape[1]
    streams = []
    size = count // len(UNIT_ORDERS)
    ub[...] = dot(gs[...], embed[...], 0, 0)
    pl.semaphore_wait(barrier, total)
    for s, order in enumerate(UNIT_ORDERS):
        own, part = s * size, size
        for axis in order:
            part //= axes[axis][2]
            own = own + where[axis] * part
        streams.append(scatter(order, ub, s * size, size, unit, own, order[::-1]))
    for stream in streams:
        next(stream)

    block = feats // n_group
    share = block // len(PROJ_ORDERS)
    cell = share // n_dp
    for g in range(n_group):
        part = dot(feat[:, g * block:(g + 1) * block], gh[...], 0, 0)
        for s, order in enumerate(PROJ_ORDERS):
            for i in range(n_dp):
                spot = {"c": i // nx, "x": i % nx, "y": g % 2, "z": g // 2}
                row = 0
                for axis in order:
                    row = row * axes[axis][2] + spot[axis]
                row = s * share * n_group + row * cell
                pb[row:row + cell] = part[s * share + i * cell:s * share + (i + 1) * cell]
    for s, order in enumerate(PROJ_ORDERS):
        size = share * n_group
        own = s * share + (c * nx + x) * cell
        stream = scatter(order, pb, s * size, size, pout, own, "xc")
        next(stream)
        streams.append(stream)

    turn = 0
    while streams:
        streams = [stream for stream in streams if next(stream, 0) is None]
        if turn == 0:
            gfeat[...] = dot(gh[...], proj[...], 1, 1).astype(BF16)
        turn += 1
    for copy in sends:
        copy.wait_send()


def sums(n_dp, n_group, grad_scores, embed_b, features, grad_hidden, proj_weight):
    count, feats, width = grad_scores.shape[1], features.shape[1], embed_b.shape[1]
    vmem = pl.BlockSpec(memory_space=pltpu.VMEM)
    n_sem = (len(UNIT_ORDERS) + len(PROJ_ORDERS)) * 2 * (4 + n_dp // 2 + n_group // 2)
    return pl.pallas_call(
        functools.partial(sums_kernel, n_dp, n_group),
        out_shape=(
            jax.ShapeDtypeStruct((count, width), F32),
            jax.ShapeDtypeStruct((feats // n_group, width), F32),
            jax.ShapeDtypeStruct(features.shape, BF16),
        ),
        in_specs=[vmem] * 5,
        out_specs=(vmem,) * 3,
        scratch_shapes=[
            pltpu.VMEM((count, width), F32),
            pltpu.VMEM((feats, width), F32),
            pltpu.VMEM((2 * (count + feats), width), F32),
            pltpu.SemaphoreType.DMA((n_sem,)),
            pltpu.SemaphoreType.DMA((n_sem,)),
        ],
        compiler_params=pltpu.CompilerParams(
            collective_id=1, has_side_effects=True, vmem_limit_bytes=48 << 20),
        name="sums",
    )(grad_scores, embed_b, features, grad_hidden, proj_weight)


def plain_sums(grad_scores, embed_b, features, grad_hidden, proj_weight):
    grad_unit = lax.psum(dot(grad_scores, embed_b, 0, 0), ("dp", "group"))
    grad_feat = dot(grad_hidden, proj_weight, 1, 1).astype(BF16)
    part = lax.psum_scatter(
        dot(features, grad_hidden, 0, 0), "group", scatter_dimension=0, tiled=True)
    return grad_unit, lax.psum(part, "dp"), grad_feat


def solution(mesh):
    n_dp, n_group = mesh.shape["dp"], mesh.shape["group"]

    def local(features, target_embed, proj_weight, prototypes):
        grad_scores, embed_b, grad_hidden = scores(
            n_dp, n_group, features, target_embed, proj_weight, prototypes)
        args = (grad_scores, embed_b, features, grad_hidden, proj_weight)
        unit = 8 * n_dp * n_group * max(len(UNIT_ORDERS), len(PROJ_ORDERS))
        even = n_dp % 2 == 0 and n_group % 2 == 0
        if even and prototypes.shape[0] % unit == 0 and features.shape[1] % unit == 0:
            grad_unit, grad_proj, grad_feat = sums(n_dp, n_group, *args)
        else:
            grad_unit, grad_proj, grad_feat = plain_sums(*args)
        scale = inv_norm(prototypes)
        unit_protos = prototypes * scale
        along = jnp.sum(unit_protos * grad_unit, axis=-1, keepdims=True)
        grad_protos = (grad_unit - unit_protos * along) * scale
        return (grad_feat, grad_proj, grad_protos)

    return jax.shard_map(
        local,
        mesh=mesh,
        in_specs=(P(("dp", "group"), None), P(("dp", "group"), None), P(), P()),
        out_specs=(P(("dp", "group"), None), P("group", None), P()),
        check_vma=False,
    )
```

```python
import functools

import jax
import jax.numpy as jnp
from jax import lax
from jax.experimental import pallas as pl
from jax.experimental.pallas import tpu as pltpu
from jax.sharding import PartitionSpec as P

SWEEPS = 3
MESH = pl.DeviceIdType.MESH
F32 = jnp.float32
BF16 = jnp.bfloat16


def normalize(values):
    return values * lax.rsqrt(jnp.sum(values * values, axis=-1, keepdims=True) + 1e-06)


def inv_norm(values):
    return lax.rsqrt(jnp.sum(values * values, axis=-1, keepdims=True) + 1e-06)


def dot(a, b, ca, cb):
    return lax.dot_general(a, b, (((ca,), (cb,)), ((), ())), preferred_element_type=F32)


def others(n, body):
    if n <= 8:
        for k in range(1, n):
            body(k)
    else:
        lax.fori_loop(1, n, lambda k, c: (body(k), c)[1], 0)


def peer_of(me, k, n):
    return lax.rem(me + k, n)


def scores_kernel(
    n_dp, n_group, feat, target, proj, protos, gs_out, embed_out, gh_out,
    kern, proto_b, slots_d, slots_g, w, hid, send_d, recv_d, send_g, recv_g,
):
    d = lax.axis_index("dp")
    g = lax.axis_index("group")
    barrier = pltpu.get_barrier_semaphore()
    others(n_dp, lambda k: pl.semaphore_signal(
        barrier, inc=1, device_id=(peer_of(d, k, n_dp), g), device_id_type=MESH))
    others(n_group, lambda k: pl.semaphore_signal(
        barrier, inc=1, device_id=(d, peer_of(g, k, n_group)), device_id_type=MESH))

    def copy_d(s, k, owner, peer):
        return pltpu.make_async_remote_copy(
            src_ref=slots_d.at[s, owner], dst_ref=slots_d.at[s, owner],
            send_sem=send_d.at[s, k], recv_sem=recv_d.at[s, owner],
            device_id=(peer, g), device_id_type=MESH)

    def copy_g(s, k, owner, peer):
        return pltpu.make_async_remote_copy(
            src_ref=slots_g.at[s, owner], dst_ref=slots_g.at[s, owner],
            send_sem=send_g.at[s, k], recv_sem=recv_g.at[s, owner],
            device_id=(d, peer), device_id_type=MESH)

    proto_b[...] = normalize(protos[...]).astype(BF16)
    target_b = normalize(target[...].astype(F32)).astype(BF16)
    kern[...] = jnp.exp(dot(target_b, proto_b[...], 1, 1) * (1.0 / 0.05))
    w[...] = jnp.ones_like(w)
    for s in range(SWEEPS):
        row = jnp.sum(kern[...] * w[...], axis=1, keepdims=True)
        slots_d[s, d] = jnp.sum(kern[...] * (1.0 / row), axis=0, keepdims=True)
        if s == 0:
            pl.semaphore_wait(barrier, n_dp - 1 + n_group - 1)
        others(n_dp, lambda k: copy_d(s, k, d, peer_of(d, k, n_dp)).start())
        if s == 0:
            hid[...] = dot(feat[...], proj[...], 1, 0)
        others(n_dp, lambda k: copy_d(s, k, peer_of(d, k, n_dp), d).wait_recv())
        slots_g[s, g] = jnp.sum(slots_d[s], axis=0)
        others(n_group, lambda k: copy_g(s, k, g, peer_of(g, k, n_group)).start())
        if s == 0:
            embed_out[...] = (hid[...] * inv_norm(hid[...])).astype(BF16)
        others(n_group, lambda k: copy_g(s, k, peer_of(g, k, n_group), g).wait_recv())
        w[...] = 1.0 / jnp.sum(slots_g[s], axis=0)
    plan = kern[...] * w[...]
    plan = plan / jnp.sum(plan, axis=1, keepdims=True)
    prob = jnp.exp(dot(embed_out[...], proto_b[...], 1, 1) * (1.0 / 0.1))
    prob = prob / jnp.sum(prob, axis=1, keepdims=True)
    gs_out[...] = ((prob - plan) * (1.0 / 0.1)).astype(BF16)
    ge = dot(gs_out[...], proto_b[...], 1, 0)
    scale = inv_norm(hid[...])
    embed = hid[...] * scale
    gh = scale * (ge - embed * jnp.sum(embed * ge, axis=-1, keepdims=True))
    gh_out[...] = gh.astype(BF16)
    for s in range(SWEEPS):
        others(n_dp, lambda k: copy_d(s, k, d, peer_of(d, k, n_dp)).wait_send())
        others(n_group, lambda k: copy_g(s, k, g, peer_of(g, k, n_group)).wait_send())


def scores(n_dp, n_group, features, target_embed, proj_weight, prototypes):
    rows = features.shape[0]
    count, width = prototypes.shape
    vmem = pl.BlockSpec(memory_space=pltpu.VMEM)
    return pl.pallas_call(
        functools.partial(scores_kernel, n_dp, n_group),
        out_shape=(
            jax.ShapeDtypeStruct((rows, count), BF16),
            jax.ShapeDtypeStruct((rows, width), BF16),
            jax.ShapeDtypeStruct((rows, width), BF16),
        ),
        in_specs=[vmem] * 4,
        out_specs=(vmem,) * 3,
        scratch_shapes=[
            pltpu.VMEM((rows, count), F32),
            pltpu.VMEM((count, width), BF16),
            pltpu.VMEM((SWEEPS, n_dp, 1, count), F32),
            pltpu.VMEM((SWEEPS, n_group, 1, count), F32),
            pltpu.VMEM((1, count), F32),
            pltpu.VMEM((rows, width), F32),
            pltpu.SemaphoreType.DMA((SWEEPS, n_dp)),
            pltpu.SemaphoreType.DMA((SWEEPS, n_dp)),
            pltpu.SemaphoreType.DMA((SWEEPS, n_group)),
            pltpu.SemaphoreType.DMA((SWEEPS, n_group)),
        ],
        compiler_params=pltpu.CompilerParams(
            collective_id=0, has_side_effects=True, vmem_limit_bytes=48 << 20),
        name="scores",
    )(features, target_embed, proj_weight, prototypes)


UNIT_ORDERS = ("cwvxy", "cwyxv", "cxwyv", "cywvx")
PROJ_ORDERS = ("cxwyv", "cxywv", "cywxv", "cywxv")
GFEAT_TURN = 7
TURNS = (
    0, 1, 2, 3, 4, 5, 6, 7, 0, 1, 2, 3, 0, 2, 3, 1, 4, 5, 0, 3, 1, 2, 6, 7, 3, 0, 1, 4, 3, 2, 0, 1, 5, 4,
    2, 0, 1, 3, 2, 4, 6, 7, 5, 1, 4, 3, 4, 0, 5, 6, 7, 2, 5, 5, 6, 7, 3, 1, 2, 3, 0, 6, 7, 1, 2, 6, 7, 0,
)


def sums_kernel(
    n_dp, n_group, gs, embed, feat, gh, proj, protos, gprotos, pout, gfeat,
    unit, ub, pb, landing, sem_s, sem_r,
):
    nx, nv = n_dp // 2, n_group // 4
    dp = lax.axis_index("dp")
    grp = lax.axis_index("group")
    x, c = dp // 2, lax.rem(dp, 2)
    z, y = grp // 2, lax.rem(grp, 2)
    v, w = z // 2, lax.rem(z, 2)
    axes = {
        "c": (lambda i: (x * 2 + i, grp), c, 2),
        "x": (lambda i: (i * 2 + c, grp), x, nx),
        "y": (lambda i: (dp, z * 2 + i), y, 2),
        "w": (lambda i: (dp, (v * 2 + i) * 2 + y), w, 2),
        "v": (lambda i: (dp, (i * 2 + w) * 2 + y), v, nv),
    }
    barrier = pltpu.get_barrier_semaphore()
    total = 0
    for at, me, n in axes.values():
        total += n - 1
        for k in range(1, n):
            pl.semaphore_signal(
                barrier, inc=1, device_id=at(peer_of(me, k, n)), device_id_type=MESH)

    used = {"sem": 0, "row": 0}
    sends = []

    def take(what, amount):
        first = used[what]
        used[what] += amount
        return first

    def start(axis, src_of, dst_of):
        at, me, n = axes[axis]
        first = take("sem", n)

        def make(k, to, sender, peer):
            return pltpu.make_async_remote_copy(
                src_ref=src_of(to), dst_ref=dst_of(sender),
                send_sem=sem_s.at[first + k], recv_sem=sem_r.at[first + sender],
                device_id=at(peer), device_id_type=MESH)

        for k in range(1, n):
            copy = make(k, peer_of(me, k, n), me, peer_of(me, k, n))
            copy.start()
            sends.append(copy)

        def wait():
            for k in range(1, n):
                other = peer_of(me, k, n)
                make(k, me, other, other).wait_recv()
        return wait

    def piece(ref, base, size):
        return ref.at[pl.ds(pl.multiple_of(base, 8), size)]

    def scatter(order, buf, base, size, out, out_base, gathered):
        for step, axis in enumerate(order):
            _, me, n = axes[axis]
            size //= n
            low, slots = base, take("row", n * size)
            wait = start(
                axis,
                lambda i, low=low, size=size: piece(buf, low + i * size, size),
                lambda j, slots=slots, size=size: piece(landing, slots + j * size, size))
            yield
            wait()
            base = low + me * size
            value = piece(buf, base, size)[...]
            for k in range(1, n):
                value = value + piece(landing, slots + peer_of(me, k, n) * size, size)[...]
            last = step == len(order) - 1
            piece(out if last else buf, out_base if last else base, size)[...] = value
        base = out_base
        for axis in gathered:
            _, me, n = axes[axis]
            low = base - me * size
            wait = start(
                axis,
                lambda i, base=base, size=size: piece(out, base, size),
                lambda j, low=low, size=size: piece(out, low + j * size, size))
            yield
            wait()
            base, size = low, size * n

    where = {"c": c, "x": x, "y": y, "w": w, "v": v}
    count, feats = gs.shape[1], feat.shape[1]
    streams = []
    size = count // len(UNIT_ORDERS)
    ub[...] = dot(gs[...], embed[...], 0, 0)
    pl.semaphore_wait(barrier, total)

    def finish(stream, low):
        yield from stream
        rows = pl.ds(low, size)
        value = protos[rows, :]
        scale = inv_norm(value)
        value = value * scale
        along = jnp.sum(value * unit[rows, :], axis=-1, keepdims=True)
        gprotos[rows, :] = (unit[rows, :] - value * along) * scale

    for s, order in enumerate(UNIT_ORDERS):
        own, part = s * size, size
        for axis in order:
            part //= axes[axis][2]
            own = own + where[axis] * part
        streams.append(finish(
            scatter(order, ub, s * size, size, unit, own, order[::-1]), s * size))
    for stream in streams:
        next(stream)

    block = feats // n_group
    share = block // len(PROJ_ORDERS)
    cell = share // n_dp
    for g in range(n_group):
        part = dot(feat[:, g * block:(g + 1) * block], gh[...], 0, 0)
        for s, order in enumerate(PROJ_ORDERS):
            for i in range(n_dp):
                spot = {"c": i // nx, "x": i % nx, "y": g % 2, "w": g // 2 % 2, "v": g // 4}
                row = 0
                for axis in order:
                    row = row * axes[axis][2] + spot[axis]
                row = s * share * n_group + row * cell
                pb[row:row + cell] = part[s * share + i * cell:s * share + (i + 1) * cell]
    for s, order in enumerate(PROJ_ORDERS):
        held = share * n_group
        own = s * share + (c * nx + x) * cell
        stream = scatter(order, pb, s * held, held, pout, own, "xc")
        next(stream)
        streams.append(stream)

    for turn, s in enumerate(TURNS):
        next(streams[s], 0)
        if turn == GFEAT_TURN:
            gfeat[...] = dot(gh[...], proj[...], 1, 1).astype(BF16)
    for copy in sends:
        copy.wait_send()


def sums(n_dp, n_group, grad_scores, embed_b, features, grad_hidden, proj_weight, prototypes):
    count, feats, width = grad_scores.shape[1], features.shape[1], embed_b.shape[1]
    vmem = pl.BlockSpec(memory_space=pltpu.VMEM)
    n_sem = (len(UNIT_ORDERS) + len(PROJ_ORDERS)) * 2 * (6 + n_dp // 2 + n_group // 4)
    return pl.pallas_call(
        functools.partial(sums_kernel, n_dp, n_group),
        out_shape=(
            jax.ShapeDtypeStruct((count, width), F32),
            jax.ShapeDtypeStruct((feats // n_group, width), F32),
            jax.ShapeDtypeStruct(features.shape, BF16),
        ),
        in_specs=[vmem] * 6,
        out_specs=(vmem,) * 3,
        scratch_shapes=[
            pltpu.VMEM((count, width), F32),
            pltpu.VMEM((count, width), F32),
            pltpu.VMEM((feats, width), F32),
            pltpu.VMEM((2 * (count + feats), width), F32),
            pltpu.SemaphoreType.DMA((n_sem,)),
            pltpu.SemaphoreType.DMA((n_sem,)),
        ],
        compiler_params=pltpu.CompilerParams(
            collective_id=1, has_side_effects=True, vmem_limit_bytes=48 << 20),
        name="sums",
    )(grad_scores, embed_b, features, grad_hidden, proj_weight, prototypes)


def plain_sums(grad_scores, embed_b, features, grad_hidden, proj_weight):
    grad_unit = lax.psum(dot(grad_scores, embed_b, 0, 0), ("dp", "group"))
    grad_feat = dot(grad_hidden, proj_weight, 1, 1).astype(BF16)
    part = lax.psum_scatter(
        dot(features, grad_hidden, 0, 0), "group", scatter_dimension=0, tiled=True)
    return grad_unit, lax.psum(part, "dp"), grad_feat


def solution(mesh):
    n_dp, n_group = mesh.shape["dp"], mesh.shape["group"]

    def local(features, target_embed, proj_weight, prototypes):
        grad_scores, embed_b, grad_hidden = scores(
            n_dp, n_group, features, target_embed, proj_weight, prototypes)
        args = (grad_scores, embed_b, features, grad_hidden, proj_weight)
        unit = 8 * n_dp * n_group * max(len(UNIT_ORDERS), len(PROJ_ORDERS))
        even = n_dp % 2 == 0 and n_group % 4 == 0
        if even and prototypes.shape[0] % unit == 0 and features.shape[1] % unit == 0:
            grad_protos, grad_proj, grad_feat = sums(n_dp, n_group, *args, prototypes)
            return (grad_feat, grad_proj, grad_protos)
        grad_unit, grad_proj, grad_feat = plain_sums(*args)
        scale = inv_norm(prototypes)
        unit_protos = prototypes * scale
        along = jnp.sum(unit_protos * grad_unit, axis=-1, keepdims=True)
        grad_protos = (grad_unit - unit_protos * along) * scale
        return (grad_feat, grad_proj, grad_protos)

    return jax.shard_map(
        local,
        mesh=mesh,
        in_specs=(P(("dp", "group"), None), P(("dp", "group"), None), P(), P()),
        out_specs=(P(("dp", "group"), None), P("group", None), P()),
        check_vma=False,
    )
```
